32 devices in a mesh: fsdp: 2 (over core), rep: 16 (over z, y, x).
Axes of the slice: x: 2, y: 2, z: 4, core: 2. Of those that a mesh axis runs over, the one named last changes fastest.
Arguments:
- tokens: bfloat16 [64, 8, 392, 512], P('rep', 'fsdp'), may hold values from -6 to 6
- grad_out: bfloat16 [64, 8, 392, 512], P('rep', 'fsdp'), may hold values from -6 to 6
- clip_ids: int32 [64], P('rep'), may hold values from 0 to 7
- norm1_gain: bfloat16 [512], replicated, may hold values from 0.5 to 1.5
- norm1_shift: bfloat16 [512], replicated, may hold values from -1 to 1
- weight_qkv: bfloat16 [512, 1536], P('fsdp'), may hold values from -0.25 to 0.25
- bias_qkv: bfloat16 [1536], replicated, may hold values from -1 to 1
- rel_table: float32 [16, 2535], replicated, may hold values from -4 to 4
- weight_out: bfloat16 [512, 512], P('fsdp'), may hold values from -0.5 to 0.5
- bias_out: bfloat16 [512], replicated, may hold values from -1 to 1
- norm2_gain: bfloat16 [512], replicated, may hold values from 0.5 to 1.5
- norm2_shift: bfloat16 [512], replicated, may hold values from -1 to 1
- weight_expand: bfloat16 [512, 2048], P('fsdp'), may hold values from -0.25 to 0.25
- bias_expand: bfloat16 [2048], replicated, may hold values from -1 to 1
- weight_reduce: bfloat16 [2048, 512], P('fsdp'), may hold values from -0.125 to 0.125
- bias_reduce: bfloat16 [512], replicated, may hold values from -1 to 1
- down_qkv: bfloat16 [512, 128], P('fsdp'), may hold values from -0.25 to 0.25
- up_qkv: bfloat16 [128, 1536], P('fsdp'), may hold values from -1.5 to 1.5
- down_out: bfloat16 [512, 128], P('fsdp'), may hold values from -0.5 to 0.5
- up_out: bfloat16 [128, 512], P('fsdp'), may hold values from -1.5 to 1.5
- down_expand: bfloat16 [512, 128], P('fsdp'), may hold values from -0.25 to 0.25
- up_expand: bfloat16 [128, 2048], P('fsdp'), may hold values from -1.5 to 1.5
- down_reduce: bfloat16 [2048, 128], P('fsdp'), may hold values from -0.125 to 0.125
- up_reduce: bfloat16 [128, 512], P('fsdp'), may hold values from -1.5 to 1.5
Outputs:
- block_out: bfloat16 [64, 8, 392, 512], P('rep', 'fsdp')
- grad_tokens: float32 [64, 8, 392, 512], P('rep', 'fsdp')
- grad_down_qkv: float32 [512, 128], P('fsdp')
- grad_up_qkv: float32 [128, 1536], P('fsdp')
- grad_down_out: float32 [512, 128], P('fsdp')
- grad_up_out: float32 [128, 512], P('fsdp')
- grad_down_expand: float32 [512, 128], P('fsdp')
- grad_up_expand: float32 [128, 2048], P('fsdp')
- grad_down_reduce: float32 [2048, 128], P('fsdp')
- grad_up_reduce: float32 [128, 512], P('fsdp')
The draws below stay inside these ranges and needn't reach their ends.
All inputs are finite; a program needn't handle non-finite values.
Results may differ from the reference program's by a relative error of at most 0.015.
The reference program's roundings to bfloat16 on the way count: a program that leaves them out, or rounds other values in their place, can miss the bound.
Values may be sent and summed in bfloat16 or wider, within the bound.
A program may use at most 832 MiB of HBM per device.

```python
import jax
import jax.numpy as jnp
from jax import lax

D = 512
HEADS = 16
HEAD_DIM = 32
FF = 2048
RANK = 16
ADAPTERS = 8
WIN_FRAMES = 8
WIN_ROWS = 7
WIN_COLS = 7
WINDOWS = 8
WIN_TOK = 392
REL_SPAN = 2535
ADAPT_COLS = 128
CLIPS = 64


def place_ends(drawn, own_key, smallest, high):
    shape = drawn.shape
    spot = [jax.random.randint(jax.random.fold_in(own_key, axis), (), 0, shape[axis]) for axis in range(len(shape))]
    drawn = drawn.at[tuple(spot)].set(smallest)
    longest = shape.index(max(shape))
    spot[longest] = (spot[longest] + 1) % shape[longest]
    return drawn.at[tuple(spot)].set(high)


def level_of(rng, extent, split, least, high):
    loudness, own = 1.0, jax.random.fold_in(rng, 6)
    for axis_at, parts in split:
        steps = jnp.exp(jax.random.uniform(jax.random.fold_in(own, axis_at), (parts,), jnp.float32, least / len(split), high / len(split)))
        loudness = loudness * jnp.repeat(steps, extent[axis_at] // parts).reshape([-1 if axis == axis_at else 1 for axis in range(len(extent))])
    return loudness


def gaussian(rng, dims, deviation, bound, pieces=(), kind=jnp.bfloat16):
    factor_of = level_of(rng, dims, pieces, -0.22, 0.18) if pieces else 1.0
    entries = jax.random.normal(rng, dims, jnp.float32) * deviation * factor_of
    return jnp.minimum(jnp.maximum(entries, -bound), bound).astype(kind)


def setup_inputs(seed: int = 0) -> dict:
    seeds = jax.random.split(jax.random.key(seed), 25)
    tokens = gaussian(seeds[0], (CLIPS, WINDOWS, WIN_TOK, D), 1.0, 6.0, ((0, 16), (1, 2)))
    grad_out = gaussian(seeds[1], (CLIPS, WINDOWS, WIN_TOK, D), 1.0, 6.0, ((0, 16), (1, 2)))
    clip_ids = place_ends(jax.random.randint(seeds[2], (CLIPS,), 0, ADAPTERS), jax.random.fold_in(seeds[2], 1), 0, ADAPTERS - 1).astype(jnp.int32)
    norm1_gain = jnp.clip(1.0 + 0.1 * jax.random.normal(seeds[3], (D,), jnp.float32), 0.5, 1.5).astype(jnp.bfloat16)
    norm1_shift = gaussian(seeds[4], (D,), 0.2, 1.0)
    weight_qkv = gaussian(seeds[5], (D, 3 * D), D ** -0.5, 0.25, ((0, 2),))
    bias_qkv = gaussian(seeds[6], (3 * D,), 0.2, 1.0)
    rel_table = gaussian(seeds[7], (HEADS, REL_SPAN), 1.0, 4.0, (), jnp.float32)
    weight_out = gaussian(seeds[8], (D, D), (D // 4) ** -0.5, 0.5, ((0, 2),))
    bias_out = gaussian(seeds[9], (D,), 0.2, 1.0)
    norm2_gain = jnp.clip(1.0 + 0.1 * jax.random.normal(seeds[10], (D,), jnp.float32), 0.5, 1.5).astype(jnp.bfloat16)
    norm2_shift = gaussian(seeds[11], (D,), 0.2, 1.0)
    weight_expand = gaussian(seeds[12], (D, FF), D ** -0.5, 0.25, ((0, 2),))
    bias_expand = gaussian(seeds[13], (FF,), 0.2, 1.0)
    weight_reduce = gaussian(seeds[14], (FF, D), FF ** -0.5, 0.125, ((0, 2),))
    bias_reduce = gaussian(seeds[15], (D,), 0.2, 1.0)
    down_qkv = gaussian(seeds[16], (D, ADAPT_COLS), D ** -0.5, 0.25, ((0, 2),))
    up_qkv = gaussian(seeds[17], (ADAPT_COLS, 3 * D), RANK ** -0.5, 1.5, ((0, 2),))
    down_out = gaussian(seeds[18], (D, ADAPT_COLS), (D // 4) ** -0.5, 0.5, ((0, 2),))
    up_out = gaussian(seeds[19], (ADAPT_COLS, D), RANK ** -0.5, 1.5, ((0, 2),))
    down_expand = gaussian(seeds[20], (D, ADAPT_COLS), D ** -0.5, 0.25, ((0, 2),))
    up_expand = gaussian(seeds[21], (ADAPT_COLS, FF), RANK ** -0.5, 1.5, ((0, 2),))
    down_reduce = gaussian(seeds[22], (FF, ADAPT_COLS), FF ** -0.5, 0.125, ((0, 2),))
    up_reduce = gaussian(seeds[23], (ADAPT_COLS, D), RANK ** -0.5, 1.5, ((0, 2),))
    return dict(tokens=tokens, grad_out=grad_out, clip_ids=clip_ids, norm1_gain=norm1_gain, norm1_shift=norm1_shift, weight_qkv=weight_qkv, bias_qkv=bias_qkv, rel_table=rel_table, weight_out=weight_out, bias_out=bias_out, norm2_gain=norm2_gain, norm2_shift=norm2_shift, weight_expand=weight_expand, bias_expand=bias_expand, weight_reduce=weight_reduce, bias_reduce=bias_reduce, down_qkv=down_qkv, up_qkv=up_qkv, down_out=down_out, up_out=up_out, down_expand=down_expand, up_expand=up_expand, down_reduce=down_reduce, up_reduce=up_reduce)


@jax.custom_vjp
def low(v):
    return lax.optimization_barrier(v.astype(jnp.bfloat16)).astype(jnp.float32)

@jax.custom_vjp
def low_back(v):
    return v

def low_keep(v):
    return (low(v), None)

def low_pass(kept, grad):
    return (grad,)

def back_keep(v):
    return (v, None)

def back_low(kept, grad):
    return (low(grad),)
low.defvjp(low_keep, low_pass)
low_back.defvjp(back_keep, back_low)

def layer_norm(values_in, norm_gain, norm_shift):
    average = lax.optimization_barrier(jnp.mean(values_in, axis=-1, keepdims=True))
    centred = values_in - average
    spread = lax.optimization_barrier(jnp.mean(centred * centred, axis=-1, keepdims=True))
    return centred * lax.rsqrt(spread + 1e-05) * norm_gain + norm_shift

def product(left, right):
    return jnp.dot(left, right, precision=lax.Precision.HIGHEST, preferred_element_type=jnp.float32)

def relative_index():
    count = WIN_FRAMES * WIN_ROWS * WIN_COLS
    place = jnp.arange(count, dtype=jnp.int32)
    frame = place // (WIN_ROWS * WIN_COLS)
    row_pos = place // WIN_COLS % WIN_ROWS
    col_pos = place % WIN_COLS
    return ((frame[:, None] - frame[None, :] + WIN_FRAMES - 1) * ((2 * WIN_ROWS - 1) * (2 * WIN_COLS - 1)) + (row_pos[:, None] - row_pos[None, :] + WIN_ROWS - 1) * (2 * WIN_COLS - 1) + (col_pos[:, None] - col_pos[None, :] + WIN_COLS - 1)).astype(jnp.int32)

def adapter_term(inputs, down, upper, adapter_mask):
    inner = low(low_back(adapter_mask * product(inputs, down)))
    return product(inner, upper)

def forward(clip_tokens, adapters, adapter_mask, frozen, position_bias):
    norm1_gain, norm1_shift, weight_qkv, bias_qkv, weight_out, bias_out, norm2_gain, norm2_shift, weight_expand, bias_expand, weight_reduce, bias_reduce = frozen
    down_qkv, up_qkv, down_out, up_out, down_expand, up_expand, down_reduce, up_reduce = adapters
    residual_in = clip_tokens.reshape(-1, D)
    first_normed = low(layer_norm(residual_in, norm1_gain, norm1_shift))
    projected = product(first_normed, weight_qkv) + bias_qkv + adapter_term(first_normed, down_qkv, up_qkv, adapter_mask)
    projected = low(low_back(projected))
    split_heads = projected.reshape(WINDOWS, WIN_TOK, 3, HEADS, HEAD_DIM)
    query_heads = split_heads[:, :, 0]
    key_heads = split_heads[:, :, 1]
    value_heads = split_heads[:, :, 2]
    raw_scores = jnp.einsum('wqhd,wkhd->whqk', query_heads, key_heads, precision=lax.Precision.HIGHEST)
    scores = low_back(raw_scores) * HEAD_DIM ** (-0.5) + position_bias[None]
    probs = jax.nn.softmax(scores, axis=-1)
    mixed = jnp.einsum('whqk,wkhd->wqhd', low(probs), value_heads, precision=lax.Precision.HIGHEST)
    mixed = low(low_back(mixed.reshape(-1, D)))
    attended = product(mixed, weight_out) + bias_out + adapter_term(mixed, down_out, up_out, adapter_mask)
    middle = residual_in + low_back(attended)
    second_normed = low(layer_norm(middle, norm2_gain, norm2_shift))
    expanded = product(second_normed, weight_expand) + bias_expand + adapter_term(second_normed, down_expand, up_expand, adapter_mask)
    expanded = low_back(expanded)
    activated = low(jax.nn.gelu(expanded, approximate=False))
    reduced = product(activated, weight_reduce) + bias_reduce + adapter_term(activated, down_reduce, up_reduce, adapter_mask)
    return middle + low_back(reduced)

def reference(tokens, grad_out, clip_ids, norm1_gain, norm1_shift, weight_qkv, bias_qkv, rel_table, weight_out, bias_out, norm2_gain, norm2_shift, weight_expand, bias_expand, weight_reduce, bias_reduce, down_qkv, up_qkv, down_out, up_out, down_expand, up_expand, down_reduce, up_reduce):
    frozen = tuple((item.astype(jnp.float32) for item in (norm1_gain, norm1_shift, weight_qkv, bias_qkv, weight_out, bias_out, norm2_gain, norm2_shift, weight_expand, bias_expand, weight_reduce, bias_reduce)))
    adapters = tuple((item.astype(jnp.float32) for item in (down_qkv, up_qkv, down_out, up_out, down_expand, up_expand, down_reduce, up_reduce)))
    position_bias = jnp.take(rel_table.astype(jnp.float32), relative_index(), axis=1)
    columns = jnp.arange(ADAPT_COLS, dtype=jnp.int32) // RANK
    masks = (clip_ids[:, None] == columns[None, :]).astype(jnp.float32)
    tokens_wide = tokens.astype(jnp.float32)
    cotangent = grad_out.astype(jnp.float32)

    def one_clip(totals, item):
        clip_tokens, clip_cot, adapter_mask = item

        def local(values_in, adapt):
            return forward(values_in, adapt, adapter_mask, frozen, position_bias)
        result, pullback = jax.vjp(local, clip_tokens, adapters)
        grad_clip, grad_adapt = pullback(clip_cot.reshape(-1, D))
        totals = jax.tree.map(jnp.add, totals, grad_adapt)
        return (totals, (result.reshape(WINDOWS, WIN_TOK, D).astype(jnp.bfloat16), grad_clip))
    start = tuple((jnp.zeros(item.shape, jnp.float32) for item in adapters))
    totals, (outputs, grad_tokens) = lax.scan(one_clip, start, (tokens_wide, cotangent, masks))
    return (outputs, grad_tokens, totals[0], totals[1], totals[2], totals[3], totals[4], totals[5], totals[6], totals[7])
```

```python
import functools

import jax
import jax.numpy as jnp
import numpy as np
from jax import lax
from jax.experimental import pallas as pl
from jax.experimental.pallas import tpu as pltpu
from jax.sharding import PartitionSpec as P

D = 512
HEADS = 16
HEAD_DIM = 32
FF = 2048
RANK = 16
COLS = 128
WIN_FRAMES = 8
WIN_ROWS = 7
WIN_COLS = 7
SPATIAL = WIN_ROWS * WIN_COLS
TOK = WIN_FRAMES * SPATIAL
SPAN_F = 2 * WIN_FRAMES - 1
SPAN_S = (2 * WIN_ROWS - 1) * (2 * WIN_COLS - 1)

HALVES = 2
HALF_HEADS = HEADS // HALVES
HALF_COLS = D // HALVES
LANES = 3200
USED = HALF_HEADS * TOK
SLOT = 384
SLOT_W = 512
CHUNK = 512
EPS = 1e-05
LOG2E = 1.4426950408889634
SCALE = HEAD_DIM ** (-0.5)

f32 = jnp.float32
bf16 = jnp.bfloat16


def dot(left, right):
    return lax.dot_general(left, right, (((1,), (0,)), ((), ())), preferred_element_type=f32)


def dot_t(left, right):
    return lax.dot_general(left, right, (((1,), (1,)), ((), ())), preferred_element_type=f32)


def chunks():
    out = []
    low = 0
    while low < LANES:
        wide = min(CHUNK, LANES - low)
        out.append((low, wide))
        low += wide
    return out


def norm_parts(rows):
    mean = jnp.sum(rows, axis=1, keepdims=True) * (1.0 / D)
    centred = rows - mean
    spread = jnp.sum(centred * centred, axis=1, keepdims=True) * (1.0 / D)
    inverse = lax.rsqrt(spread + EPS)
    return centred * inverse, inverse


def norm_back(grad_rows, gain, normed, inverse):
    scaled = grad_rows * gain
    first = jnp.sum(scaled, axis=1, keepdims=True) * (1.0 / D)
    second = jnp.sum(scaled * normed, axis=1, keepdims=True) * (1.0 / D)
    return inverse * (scaled - first - normed * second)


def widen(rows):
    return jnp.concatenate(
        [rows, jnp.zeros((rows.shape[0], SLOT_W - rows.shape[1]), rows.dtype)], axis=1
    )


def spread_heads(rows_t, block_ref, half):
    for j in range(HALF_HEADS):
        piece = rows_t[j * HEAD_DIM : (j + 1) * HEAD_DIM]
        if j:
            piece = pltpu.roll(piece, 8 * j, 1)
        block_ref[
            half, j * HEAD_DIM : (j + 1) * HEAD_DIM, SLOT * j : SLOT * j + SLOT_W
        ] = piece


def heads_of(low, wide):
    first = min(low // TOK, HALF_HEADS - 1)
    last = min((low + wide - 1) // TOK, HALF_HEADS - 1)
    return first, last


def pick_heads(product, low, wide, first, last):
    lane = lax.broadcasted_iota(jnp.int32, (HEAD_DIM, wide), 1) + low
    result = product[0:HEAD_DIM]
    for head in range(first + 1, last + 1):
        at = (head - first) * HEAD_DIM
        result = jnp.where(lane >= head * TOK, product[at : at + HEAD_DIM], result)
    return result


def merge(weight_ref, down_ref, up_ref, out_ref, adapter):
    rows, cols = weight_ref.shape
    down = down_ref[...]
    owner = lax.broadcasted_iota(jnp.int32, (COLS, 512), 0) // RANK
    for low in range(0, cols, 512):
        part = up_ref[:, low : low + 512]
        part = jnp.where(owner == adapter, part.astype(f32), 0.0).astype(bf16)
        for top in range(0, rows, 512):
            both = weight_ref[top : top + 512, low : low + 512].astype(f32) + dot(
                down[top : top + 512], part
            )
            out_ref[top : top + 512, low : low + 512] = both.astype(bf16)


def bias_kernel(table_ref, select_ref, out_ref, rows_ref):
    half = pl.program_id(0)
    j = pl.program_id(1)
    group = 5

    @pl.when((half == 0) & (j == 0))
    def _():
        place = lax.broadcasted_iota(jnp.int32, (256, group * SPATIAL), 0)
        table = table_ref[...]
        high = table.astype(bf16)
        rest = table - high.astype(f32)
        middle = rest.astype(bf16)
        low = (rest - middle.astype(f32)).astype(bf16)
        for g in range(10):
            hot = jnp.where(place == select_ref[g : g + 1, :], 1.0, 0.0).astype(bf16)
            found = dot(high, hot) + dot(middle, hot) + dot(low, hot)
            for s in range(group):
                sj = g * group + s
                if sj < SPATIAL:
                    pieces = [
                        found[k * HEADS : (k + 1) * HEADS, s * SPATIAL : (s + 1) * SPATIAL]
                        for k in range(SPAN_F)
                    ]
                    pieces.append(jnp.zeros((HEADS, 768 - SPAN_F * SPATIAL), f32))
                    line = jnp.concatenate(pieces, axis=1) * LOG2E
                    for at in range(6):
                        rows_ref[at, sj * HEADS : (sj + 1) * HEADS, :] = line[
                            :, at * 128 : (at + 1) * 128
                        ]

    @pl.when(j == 0)
    def _():
        out_ref[...] = jnp.zeros_like(out_ref)

    head = half * HALF_HEADS + j
    rows = jnp.concatenate(
        [rows_ref[at, pl.ds(head, SPATIAL, stride=HEADS), :] for at in range(6)], axis=1
    )
    parts = []
    for fj in range(WIN_FRAMES):
        low = (WIN_FRAMES - 1 - fj) * SPATIAL
        parts.append(rows[:, low : low + TOK])
    whole = widen(jnp.concatenate(parts, axis=0))
    for at in range(HALF_HEADS):

        @pl.when(j == at)
        def _():
            piece = pltpu.roll(whole, 8 * at, 1) if at else whole
            out_ref[0, :, SLOT * at : SLOT * at + SLOT_W] += piece


def bias_tables(rel_table):
    table = rel_table.reshape(HEADS, SPAN_F, SPAN_S).transpose(1, 0, 2)
    table = jnp.pad(table.reshape(SPAN_F * HEADS, SPAN_S), ((0, 0), (0, 256 - SPAN_S)))
    spot = np.arange(SPATIAL)
    flat = spot // WIN_COLS * (2 * WIN_COLS - 1) + spot % WIN_COLS
    centre = (WIN_ROWS - 1) * (2 * WIN_COLS - 1) + WIN_COLS - 1
    pairs = flat[None, :] - flat[:, None] + centre
    pairs = np.concatenate([pairs, np.zeros((1, SPATIAL), pairs.dtype)], axis=0)
    select = jnp.asarray(pairs.reshape(10, 5 * SPATIAL), jnp.int32)
    return pl.pallas_call(
        bias_kernel,
        grid=(HALVES, HALF_HEADS),
        in_specs=[
            pl.BlockSpec((SPAN_F * HEADS, 256), lambda a, b: (0, 0)),
            pl.BlockSpec((10, 5 * SPATIAL), lambda a, b: (0, 0)),
        ],
        out_specs=pl.BlockSpec((1, TOK, LANES), lambda a, b: (a, 0, 0)),
        out_shape=jax.ShapeDtypeStruct((HALVES, TOK, LANES), f32),
        scratch_shapes=[pltpu.VMEM((6, SPATIAL * HEADS, 128), f32)],
        compiler_params=pltpu.CompilerParams(vmem_limit_bytes=40 << 20),
        name="bias_tables",
    )(table, select)


def outer_kernel(
    wins,
    ids,
    x_ref,
    g_ref,
    gain1,
    shift1,
    gain2,
    shift2,
    w_qkv,
    b_qkv,
    w_out,
    b_out,
    w_exp,
    b_exp,
    w_red,
    b_red,
    d_qkv,
    u_qkv,
    d_out,
    u_out,
    d_exp,
    u_exp,
    d_red,
    u_red,
    bias,
    block_out,
    p_out,
    qt_out,
    kt_out,
    v_out,
    dot_out,
    row_out,
    dx1_out,
    h1_out,
    u1_out,
    acc_do,
    acc_uo,
    acc_de,
    acc_ue,
    acc_dr,
    acc_ur,
    m_qkv,
    m_out,
    m_exp,
    m_red,
    t_qkv,
    t_out,
    t_exp,
    t_red,
    q_block,
    o_t,
    o_flat,
    k_ref,
    vt_ref,
):
    step = pl.program_id(0)
    adapter = ids[step // wins]
    mine = pl.ds(pl.multiple_of(adapter * RANK, RANK), RANK)

    @pl.when(step == 0)
    def _():
        q_block[...] = jnp.zeros_like(q_block)
        t_qkv[...] = d_qkv[...].T
        t_out[...] = d_out[...].T
        t_exp[...] = d_exp[...].T
        t_red[...] = d_red[...].T
        for ref in (acc_do, acc_uo, acc_de, acc_ue, acc_dr, acc_ur):
            ref[...] = jnp.zeros_like(ref)

    @pl.when(lax.rem(step, wins) == 0)
    def _():
        merge(w_qkv, d_qkv, u_qkv, m_qkv, adapter)
        merge(w_out, d_out, u_out, m_out, adapter)
        merge(w_exp, d_exp, u_exp, m_exp, adapter)
        merge(w_red, d_red, u_red, m_red, adapter)

    x = x_ref[0].astype(f32)
    normed, _ = norm_parts(x)
    h1 = (normed * gain1[...] + shift1[...]).astype(bf16)
    h1_out[0] = h1
    u1_out[0] = dot_t(t_qkv[mine, :], h1).astype(bf16)
    q = (dot(h1, m_qkv[:, 0:D]) + b_qkv[:, 0:D]).astype(bf16)
    k = (dot(h1, m_qkv[:, D : 2 * D]) + b_qkv[:, D : 2 * D]).astype(bf16)
    v = (dot(h1, m_qkv[:, 2 * D :]) + b_qkv[:, 2 * D :]).astype(bf16)
    v_out[0] = v
    k_ref[...] = k
    q_t = widen(q.T)
    qt_out[0] = q_t
    for half in range(HALVES):
        spread_heads(q_t[half * HALF_COLS : (half + 1) * HALF_COLS], q_block, half)
    kt_out[0] = k.T
    vt_ref[...] = v.T

    for half in range(HALVES):
        own = slice(half * HALF_COLS, (half + 1) * HALF_COLS)
        for low, wide in chunks():
            span = slice(low, low + wide)
            scores = dot(k_ref[:, own], q_block[half, :, span]) * (SCALE * LOG2E)
            scores = scores + bias[half, :, span]
            top = jnp.max(scores, axis=0, keepdims=True)
            power = jnp.exp2(scores - top)
            total = jnp.sum(power, axis=0, keepdims=True)
            probs = (power * (1.0 / total)).astype(bf16)
            p_out[0, half, :, span] = probs
            first, last = heads_of(low, wide)
            rows = slice(
                half * HALF_COLS + first * HEAD_DIM, half * HALF_COLS + (last + 1) * HEAD_DIM
            )
            o_flat[half, :, span] = pick_heads(dot(vt_ref[rows, :], probs), low, wide, first, last)
    for half in range(HALVES):
        for j in range(HALF_HEADS):
            piece = o_flat[half, :, SLOT * j : SLOT * j + SLOT_W]
            if j:
                piece = pltpu.roll(piece, SLOT_W - 8 * j, 1)
            at = half * HALF_COLS + j * HEAD_DIM
            o_t[at : at + HEAD_DIM, :] = piece
    o_tb = o_t[...].astype(bf16)
    o = o_tb.T[0:TOK]

    u2 = dot(t_out[mine, :], o_tb[:, 0:TOK]).astype(bf16)
    x1 = x + dot(o, m_out[...]) + b_out[...]
    normed2, inverse2 = norm_parts(x1)
    h2 = (normed2 * gain2[...] + shift2[...]).astype(bf16)
    u3 = dot_t(t_exp[mine, :], h2).astype(bf16)
    dz = g_ref[0]
    g = dz.astype(f32)
    du4 = dot_t(u_red[mine, :], dz).astype(bf16)
    z = x1 + b_red[...]
    dh2 = jnp.zeros((TOK, D), f32)
    u4 = jnp.zeros((RANK, TOK), f32)
    du3 = jnp.zeros((RANK, TOK), f32)
    for low in range(0, FF, 512):
        span = slice(low, low + 512)
        f = dot(h2, m_exp[:, span]) + b_exp[:, span]
        phi = 0.5 + 0.5 * lax.erf(f * (2.0**-0.5))
        act = (f * phi).astype(bf16)
        slope = phi + f * (jnp.exp2(f * f * (-0.5 * LOG2E)) * 0.3989422804014327)
        da = dot_t(dz, m_red[span, :])
        df = (da * slope).astype(bf16)
        z = z + dot(act, m_red[span, :])
        dh2 = dh2 + dot_t(df, m_exp[:, span])
        u4 = u4 + dot_t(t_red[mine, span], act)
        du3 = du3 + dot_t(u_exp[mine, span], df)
        acc_dr[mine, span] += dot(du4, act)
        acc_ue[mine, span] += dot(u3, df)
    block_out[0] = z.astype(bf16)
    acc_ur[mine, :] += dot(u4.astype(bf16), dz)
    acc_de[mine, :] += dot(du3.astype(bf16), h2)
    dx1 = g + norm_back(dh2, gain2[...], normed2, inverse2)
    dx1_out[0] = dx1
    dy = dx1.astype(bf16)
    acc_uo[mine, :] += dot(u2, dy)
    du2 = dot_t(u_out[mine, :], dy).astype(bf16)
    acc_do[mine, :] += dot(du2, o)
    d_ot = widen(dot_t(m_out[...], dy).astype(bf16))
    dot_out[0] = d_ot
    both = d_ot.astype(f32) * o_t[...]
    sums = jnp.sum(both.reshape(HEADS, HEAD_DIM, SLOT_W), axis=1)
    row_out[0] = sums


def inner_kernel(
    wins,
    ids,
    x_ref,
    gain1,
    w_qkv,
    d_qkv,
    u_qkv,
    p_ref,
    qt_ref,
    kt_ref,
    v_ref,
    dot_ref,
    row_ref,
    dx1_ref,
    h1_ref,
    u1_ref,
    grad_out,
    acc_dq,
    acc_uq,
    m_qkv,
    q_block,
    o_block,
    ds_ref,
    dq_flat,
    dq_t,
    row_flat,
    dqkv,
):
    step = pl.program_id(0)
    adapter = ids[step // wins]
    mine = pl.ds(pl.multiple_of(adapter * RANK, RANK), RANK)

    @pl.when(step == 0)
    def _():
        q_block[...] = jnp.zeros_like(q_block)
        o_block[...] = jnp.zeros_like(o_block)
        acc_dq[...] = jnp.zeros_like(acc_dq)
        acc_uq[...] = jnp.zeros_like(acc_uq)

    @pl.when(lax.rem(step, wins) == 0)
    def _():
        merge(w_qkv, d_qkv, u_qkv, m_qkv, adapter)

    row_flat[...] = jnp.zeros_like(row_flat)
    for half in range(HALVES):
        own = slice(half * HALF_COLS, (half + 1) * HALF_COLS)
        spread_heads(qt_ref[0, own, :], q_block, half)
        spread_heads(dot_ref[0, own, :], o_block, half)
        for j in range(HALF_HEADS):
            at = half * HALF_HEADS + j
            piece = row_ref[0, at : at + 1, :]
            if j:
                piece = pltpu.roll(piece, 8 * j, 1)
            row_flat[half : half + 1, SLOT * j : SLOT * j + SLOT_W] += piece

    for half in range(HALVES):
        own = slice(half * HALF_COLS, (half + 1) * HALF_COLS)
        for low, wide in chunks():
            span = slice(low, low + wide)
            d_probs = dot(v_ref[0, :, own], o_block[half, :, span])
            probs = p_ref[0, half, :, span].astype(f32)
            d_scores = (probs * (d_probs - row_flat[half : half + 1, span])).astype(bf16)
            ds_ref[:, span] = d_scores
            first, last = heads_of(low, wide)
            rows = slice(
                half * HALF_COLS + first * HEAD_DIM, half * HALF_COLS + (last + 1) * HEAD_DIM
            )
            dq_flat[half, :, span] = pick_heads(
                dot(kt_ref[0, rows, :], d_scores), low, wide, first, last
            )
        at = slice(2 * D + half * HALF_COLS, 2 * D + (half + 1) * HALF_COLS)
        dqkv[:, at] = dot_t(p_ref[0, half], o_block[half]).astype(bf16)
        at = slice(D + half * HALF_COLS, D + (half + 1) * HALF_COLS)
        dqkv[:, at] = (dot_t(ds_ref[...], q_block[half]) * SCALE).astype(bf16)
        for j in range(HALF_HEADS):
            piece = dq_flat[half, :, SLOT * j : SLOT * j + SLOT_W] * SCALE
            if j:
                piece = pltpu.roll(piece, SLOT_W - 8 * j, 1)
            at = half * HALF_COLS + j * HEAD_DIM
            dq_t[at : at + HEAD_DIM, :] = piece.astype(bf16)
    dqkv[:, 0:D] = dq_t[...].T[0:TOK]

    whole = dqkv[...]
    acc_uq[mine, :] += dot(u1_ref[0], whole)
    du1 = dot_t(u_qkv[mine, :], whole).astype(bf16)
    acc_dq[mine, :] += dot(du1, h1_ref[0])
    dh1 = dot_t(whole, m_qkv[...])
    normed, inverse = norm_parts(x_ref[0].astype(f32))
    grad_out[0] = dx1_ref[0] + norm_back(dh1, gain1[...], normed, inverse)


def whole_spec(shape):
    return pl.BlockSpec(shape, lambda i, ids: (0,) * len(shape), pipeline_mode=pl.Buffered(1))


def step_spec(shape):
    return pl.BlockSpec((1,) + shape, lambda i, ids: (i,) + (0,) * len(shape))


def block_pass(wins, tokens, grads, ids, vectors, weights, adapters, rel_table):
    groups = tokens.shape[0]
    gain1, shift1, gain2, shift2, b_qkv, b_out, b_exp, b_red = [
        item.astype(f32).reshape(1, -1) for item in vectors
    ]
    w_qkv, w_out, w_exp, w_red = weights
    d_qkv, u_qkv, d_out, u_out, d_exp, u_exp, d_red, u_red = adapters
    bias = bias_tables(rel_table)
    fixed = (
        gain1,
        shift1,
        gain2,
        shift2,
        w_qkv,
        b_qkv,
        w_out,
        b_out,
        w_exp,
        b_exp,
        w_red,
        b_red,
        d_qkv,
        u_qkv,
        d_out,
        u_out,
        d_exp,
        u_exp,
        d_red,
        u_red,
        bias,
    )
    per_step = [
        ((TOK, D), bf16),
        ((HALVES, TOK, LANES), bf16),
        ((D, SLOT_W), bf16),
        ((D, TOK), bf16),
        ((TOK, D), bf16),
        ((D, SLOT_W), bf16),
        ((HEADS, SLOT_W), f32),
        ((TOK, D), f32),
        ((TOK, D), bf16),
        ((RANK, TOK), bf16),
    ]
    sums = [D, D, D, FF, FF, D]
    outs = pl.pallas_call(
        functools.partial(outer_kernel, wins),
        grid_spec=pltpu.PrefetchScalarGridSpec(
            num_scalar_prefetch=1,
            grid=(groups,),
            in_specs=[step_spec((TOK, D))] * 2 + [whole_spec(item.shape) for item in fixed],
            out_specs=[step_spec(shape) for shape, _ in per_step]
            + [whole_spec((COLS, wide)) for wide in sums],
            scratch_shapes=[
                pltpu.VMEM((D, 3 * D), bf16),
                pltpu.VMEM((D, D), bf16),
                pltpu.VMEM((D, FF), bf16),
                pltpu.VMEM((FF, D), bf16),
                pltpu.VMEM((COLS, D), bf16),
                pltpu.VMEM((COLS, D), bf16),
                pltpu.VMEM((COLS, D), bf16),
                pltpu.VMEM((COLS, FF), bf16),
                pltpu.VMEM((HALVES, HALF_COLS, LANES), bf16),
                pltpu.VMEM((D, SLOT_W), f32),
                pltpu.VMEM((HALVES, HEAD_DIM, LANES), f32),
                pltpu.VMEM((TOK, D), bf16),
                pltpu.VMEM((D, TOK), bf16),
            ],
        ),
        out_shape=[jax.ShapeDtypeStruct((groups,) + shape, kind) for shape, kind in per_step]
        + [jax.ShapeDtypeStruct((COLS, wide), f32) for wide in sums],
        compiler_params=pltpu.CompilerParams(vmem_limit_bytes=63 << 20),
        name="outer_pass",
    )(ids, tokens, grads, *fixed)
    block_out, probs, q_t, k_t, v, d_ot, rows, dx1, h1, u1 = outs[:10]
    acc_do, acc_uo, acc_de, acc_ue, acc_dr, acc_ur = outs[10:]
    small = (gain1, w_qkv, d_qkv, u_qkv)
    grad_tokens, acc_dq, acc_uq = pl.pallas_call(
        functools.partial(inner_kernel, wins),
        grid_spec=pltpu.PrefetchScalarGridSpec(
            num_scalar_prefetch=1,
            grid=(groups,),
            in_specs=[step_spec((TOK, D))]
            + [whole_spec(item.shape) for item in small]
            + [step_spec(shape) for shape, _ in per_step[1:]],
            out_specs=[step_spec((TOK, D)), whole_spec((COLS, D)), whole_spec((COLS, 3 * D))],
            scratch_shapes=[
                pltpu.VMEM((D, 3 * D), bf16),
                pltpu.VMEM((HALVES, HALF_COLS, LANES), bf16),
                pltpu.VMEM((HALVES, HALF_COLS, LANES), bf16),
                pltpu.VMEM((TOK, LANES), bf16),
                pltpu.VMEM((HALVES, HEAD_DIM, LANES), f32),
                pltpu.VMEM((D, SLOT_W), bf16),
                pltpu.VMEM((HALVES, LANES), f32),
                pltpu.VMEM((TOK, 3 * D), bf16),
            ],
        ),
        out_shape=[
            jax.ShapeDtypeStruct((groups, TOK, D), f32),
            jax.ShapeDtypeStruct((COLS, D), f32),
            jax.ShapeDtypeStruct((COLS, 3 * D), f32),
        ],
        compiler_params=pltpu.CompilerParams(vmem_limit_bytes=63 << 20),
        name="inner_pass",
    )(ids, tokens, *small, probs, q_t, k_t, v, d_ot, rows, dx1, h1, u1)
    return (
        block_out,
        grad_tokens,
        (acc_dq, acc_uq, acc_do, acc_uo, acc_de, acc_ue, acc_dr, acc_ur),
    )


def on_device(
    tokens,
    grad_out,
    clip_ids,
    norm1_gain,
    norm1_shift,
    weight_qkv,
    bias_qkv,
    rel_table,
    weight_out,
    bias_out,
    norm2_gain,
    norm2_shift,
    weight_expand,
    bias_expand,
    weight_reduce,
    bias_reduce,
    down_qkv,
    up_qkv,
    down_out,
    up_out,
    down_expand,
    up_expand,
    down_reduce,
    up_reduce,
):
    clips, wins, length, width = tokens.shape
    shape = tokens.shape

    def full(item):
        return lax.all_gather(item, "fsdp", axis=0, tiled=True)

    block_out, grad_tokens, sums = block_pass(
        wins,
        tokens.reshape(clips * wins, length, width),
        grad_out.reshape(clips * wins, length, width),
        clip_ids,
        (
            norm1_gain,
            norm1_shift,
            norm2_gain,
            norm2_shift,
            bias_qkv,
            bias_out,
            bias_expand,
            bias_reduce,
        ),
        tuple(full(item) for item in (weight_qkv, weight_out, weight_expand, weight_reduce)),
        tuple(
            full(item)
            for item in (
                down_qkv,
                up_qkv,
                down_out,
                up_out,
                down_expand,
                up_expand,
                down_reduce,
                up_reduce,
            )
        ),
        rel_table,
    )
    totals = lax.psum(sums, ("fsdp", "rep"))
    member = lax.axis_index("fsdp")
    members = lax.axis_size("fsdp")
    shares = []
    for at, entire in enumerate(totals):
        if at % 2 == 0:
            part = entire.shape[1] // members
            shares.append(lax.dynamic_slice_in_dim(entire, member * part, part, 1).T)
        else:
            part = entire.shape[0] // members
            shares.append(lax.dynamic_slice_in_dim(entire, member * part, part, 0))
    return (block_out.reshape(shape), grad_tokens.reshape(shape), *shares)


def solution(mesh):
    row = P("fsdp", None)
    tokens = P("rep", "fsdp", None, None)
    in_specs = (
        tokens,
        tokens,
        P("rep"),
        P(),
        P(),
        row,
        P(),
        P(),
        row,
        P(),
        P(),
        P(),
        row,
        P(),
        row,
        P(),
    ) + (row,) * 8
    out_specs = (tokens, tokens) + (row,) * 8
    return jax.shard_map(
        on_device, mesh=mesh, in_specs=in_specs, out_specs=out_specs, check_vma=False
    )
```

```python
import functools

import jax
import jax.numpy as jnp
import numpy as np
from jax import lax
from jax.experimental import pallas as pl
from jax.experimental.pallas import tpu as pltpu
from jax.sharding import PartitionSpec as P

D = 512
HEADS = 16
HEAD_DIM = 32
FF = 2048
RANK = 16
COLS = 128
WIN_FRAMES = 8
WIN_ROWS = 7
WIN_COLS = 7
SPATIAL = WIN_ROWS * WIN_COLS
TOK = WIN_FRAMES * SPATIAL
SPAN_F = 2 * WIN_FRAMES - 1
SPAN_S = (2 * WIN_ROWS - 1) * (2 * WIN_COLS - 1)

HALVES = 2
HALF_HEADS = HEADS // HALVES
HALF_COLS = D // HALVES
LANES = 3200
USED = HALF_HEADS * TOK
SLOT = 384
SLOT_W = 512
OUTER_WIDTHS = (640,) * 5
INNER_WIDTHS = (768, 768, 768, 896)
EPS = 1e-05
LOG2E = 1.4426950408889634
SCALE = HEAD_DIM ** (-0.5)
VECTORS = (D, D, D, D, 3 * D, D, FF, D)
GROUP = 5
OUTER = ((D, D), (D, FF), (FF, D))
INNER = ((D, 3 * D),)

f32 = jnp.float32
bf16 = jnp.bfloat16


def dot(left, right):
    return lax.dot_general(left, right, (((1,), (0,)), ((), ())), preferred_element_type=f32)


def dot_t(left, right):
    return lax.dot_general(left, right, (((1,), (1,)), ((), ())), preferred_element_type=f32)


def chunks(widths):
    out = []
    low = 0
    for wide in widths:
        out.append((low, wide))
        low += wide
    return out


def norm_parts(rows):
    mean = jnp.sum(rows, axis=1, keepdims=True) * (1.0 / D)
    centred = rows - mean
    spread = jnp.sum(centred * centred, axis=1, keepdims=True) * (1.0 / D)
    inverse = lax.rsqrt(spread + EPS)
    return centred * inverse, inverse


def norm_back(grad_rows, gain, normed, inverse):
    scaled = grad_rows * gain
    first = jnp.sum(scaled, axis=1, keepdims=True) * (1.0 / D)
    second = jnp.sum(scaled * normed, axis=1, keepdims=True) * (1.0 / D)
    return inverse * (scaled - first - normed * second)


def widen(rows):
    return jnp.concatenate(
        [rows, jnp.zeros((rows.shape[0], SLOT_W - rows.shape[1]), rows.dtype)], axis=1
    )


def spread_heads(rows_t, block_ref, half):
    for j in range(HALF_HEADS):
        piece = rows_t[j * HEAD_DIM : (j + 1) * HEAD_DIM]
        if j:
            piece = pltpu.roll(piece, 8 * j, 1)
        block_ref[
            half, j * HEAD_DIM : (j + 1) * HEAD_DIM, SLOT * j : SLOT * j + SLOT_W
        ] = piece


def heads_of(low, wide):
    first = min(low // TOK, HALF_HEADS - 1)
    last = min((low + wide - 1) // TOK, HALF_HEADS - 1)
    return first, last


def pick_heads(product, low, wide, first, last):
    lane = lax.broadcasted_iota(jnp.int32, (HEAD_DIM, wide), 1) + low
    result = product[0:HEAD_DIM]
    for head in range(first + 1, last + 1):
        at = (head - first) * HEAD_DIM
        result = jnp.where(lane >= head * TOK, product[at : at + HEAD_DIM], result)
    return result


def unpack_vectors(vectors):
    out = []
    low = 0
    for wide in VECTORS:
        out.append(vectors.at[:, low : low + wide])
        low += wide
    return out


def pack_sums(sums_out, members, sums):
    at = 0
    flipped = [ref[...].T for ref in sums[::2]]
    for member in range(members):
        for down, up_ref in zip(flipped, sums[1::2]):
            part = down.shape[0] // members
            sums_out[at : at + part, :] = down[member * part : (member + 1) * part]
            at += part
            part = COLS // members
            for low in range(0, up_ref.shape[1], 128):
                sums_out[at : at + part, :] = up_ref[
                    member * part : (member + 1) * part, low : low + 128
                ]
                at += part


def merge(weight_ref, down_ref, up_ref, out_ref, adapter):
    rows, cols = weight_ref.shape
    down = down_ref[...]
    owner = lax.broadcasted_iota(jnp.int32, (COLS, 512), 0) // RANK
    for low in range(0, cols, 512):
        part = up_ref[:, low : low + 512]
        part = jnp.where(owner == adapter, part.astype(f32), 0.0).astype(bf16)
        for top in range(0, rows, 512):
            both = weight_ref[top : top + 512, low : low + 512].astype(f32) + dot(
                down[top : top + 512], part
            )
            out_ref[top : top + 512, low : low + 512] = both.astype(bf16)


def bias_rows(table_ref, select_ref, rows_ref):
    place = lax.broadcasted_iota(jnp.int32, (256, GROUP * SPATIAL), 0)
    table = jnp.concatenate(
        [table_ref[:, k * SPAN_S : (k + 1) * SPAN_S] for k in range(SPAN_F)], axis=0
    )
    table = jnp.concatenate(
        [table, jnp.zeros((SPAN_F * HEADS, 256 - SPAN_S), f32)], axis=1
    )
    high = table.astype(bf16)
    rest = table - high.astype(f32)
    middle = rest.astype(bf16)
    low = (rest - middle.astype(f32)).astype(bf16)
    for g in range(10):
        hot = jnp.where(place == select_ref[g : g + 1, :], 1.0, 0.0).astype(bf16)
        found = (dot(high, hot) + dot(middle, hot) + dot(low, hot)) * LOG2E
        for s in range(GROUP):
            sj = g * GROUP + s
            if sj < SPATIAL:
                pieces = [
                    found[k * HEADS : (k + 1) * HEADS, s * SPATIAL : (s + 1) * SPATIAL]
                    for k in range(SPAN_F)
                ]
                pieces.append(jnp.zeros((HEADS, 768 - SPAN_F * SPATIAL), f32))
                line = jnp.concatenate(pieces, axis=1)
                for at in range(6):
                    rows_ref[at, sj * HEADS : (sj + 1) * HEADS, :] = line[
                        :, at * 128 : (at + 1) * 128
                    ]


def bias_half(rows_ref, out_ref, half):
    lane = lax.broadcasted_iota(jnp.int32, (TOK, SLOT_W), 1)
    for j in range(HALF_HEADS):
        head = half * HALF_HEADS + j
        rows = jnp.concatenate(
            [rows_ref[at, pl.ds(head, SPATIAL, stride=HEADS), :] for at in range(6)], axis=1
        )
        parts = []
        for fj in range(WIN_FRAMES):
            shift = (8 * j - (WIN_FRAMES - 1 - fj) * SPATIAL) % 768
            part = pltpu.roll(rows, shift, 1) if shift else rows
            parts.append(part[:, 0:SLOT_W])
        piece = jnp.concatenate(parts, axis=0)
        piece = jnp.where((lane >= 8 * j) & (lane < 8 * j + TOK), piece, 0.0)
        low = SLOT * j
        if j:
            out_ref[half, :, low : low + 128] += piece[:, 0:128]
        else:
            out_ref[half, :, low : low + 128] = piece[:, 0:128]
        out_ref[half, :, low + 128 : low + SLOT_W] = piece[:, 128:]


def select_rows():
    spot = np.arange(SPATIAL)
    flat = spot // WIN_COLS * (2 * WIN_COLS - 1) + spot % WIN_COLS
    centre = (WIN_ROWS - 1) * (2 * WIN_COLS - 1) + WIN_COLS - 1
    pairs = flat[None, :] - flat[:, None] + centre
    pairs = np.concatenate([pairs, np.zeros((1, SPATIAL), pairs.dtype)], axis=0)
    return jnp.asarray(pairs.reshape(10, GROUP * SPATIAL), jnp.int32)


def bias_only_kernel(table_ref, select_ref, out_ref, rows_ref):
    bias_rows(table_ref, select_ref, rows_ref)
    for half in range(HALVES):
        bias_half(rows_ref, out_ref, half)


def bias_tables(rel_table):
    return pl.pallas_call(
        bias_only_kernel,
        in_specs=[pl.BlockSpec(memory_space=pltpu.VMEM)] * 2,
        out_specs=pl.BlockSpec(memory_space=pltpu.VMEM),
        out_shape=jax.ShapeDtypeStruct((HALVES, TOK, LANES), f32),
        scratch_shapes=[pltpu.VMEM((6, SPATIAL * HEADS, 128), f32)],
        compiler_params=pltpu.CompilerParams(vmem_limit_bytes=40 << 20),
        name="bias_tables",
    )(rel_table, select_rows())


def outer_kernel(
    wins,
    members,
    ids,
    x_ref,
    g_ref,
    vectors,
    w_qkv,
    w_out,
    w_exp,
    w_red,
    d_qkv,
    u_qkv,
    d_out,
    u_out,
    d_exp,
    u_exp,
    d_red,
    u_red,
    bias,
    block_out,
    p_out,
    qt_out,
    kt_out,
    v_out,
    dot_out,
    row_out,
    dx1_out,
    h1_out,
    u1_out,
    sums_out,
    acc_do,
    acc_uo,
    acc_de,
    acc_ue,
    acc_dr,
    acc_ur,
    m_qkv,
    m_out,
    m_exp,
    m_red,
    t_qkv,
    t_out,
    t_exp,
    t_red,
    q_block,
    o_t,
    o_flat,
    i_flat,
    i_t,
    k_ref,
    vt_ref,
):
    step = pl.program_id(0)
    adapter = ids[step // wins]
    mine = pl.ds(pl.multiple_of(adapter * RANK, RANK), RANK)
    gain1, shift1, gain2, shift2, b_qkv, b_out, b_exp, b_red = unpack_vectors(vectors)

    @pl.when(step == 0)
    def _():
        q_block[...] = jnp.zeros_like(q_block)
        t_qkv[...] = d_qkv[...].T
        t_out[...] = d_out[...].T
        t_exp[...] = d_exp[...].T
        t_red[...] = d_red[...].T
        for ref in (acc_do, acc_uo, acc_de, acc_ue, acc_dr, acc_ur):
            ref[...] = jnp.zeros_like(ref)

    @pl.when(lax.rem(step, wins) == 0)
    def _():
        merge(w_qkv, d_qkv, u_qkv, m_qkv, adapter)
        merge(w_out, d_out, u_out, m_out, adapter)
        m_out[D : D + RANK, :] = u_out[mine, :]
        merge(w_exp, d_exp, u_exp, m_exp, adapter)
        merge(w_red, d_red, u_red, m_red, adapter)

    x = x_ref[0].astype(f32)
    normed, _ = norm_parts(x)
    h1 = (normed * gain1[...] + shift1[...]).astype(bf16)
    h1_out[0] = h1
    u1_out[0] = dot_t(t_qkv[mine, :], h1).astype(bf16)
    q = (dot(h1, m_qkv[:, 0:D]) + b_qkv[:, 0:D]).astype(bf16)
    k = (dot(h1, m_qkv[:, D : 2 * D]) + b_qkv[:, D : 2 * D]).astype(bf16)
    v = (dot(h1, m_qkv[:, 2 * D :]) + b_qkv[:, 2 * D :]).astype(bf16)
    v_out[0] = v
    k_ref[...] = k
    q_t = widen(q.T)
    qt_out[0] = q_t
    for half in range(HALVES):
        spread_heads(q_t[half * HALF_COLS : (half + 1) * HALF_COLS], q_block, half)
    kt_out[0] = k.T
    vt_ref[...] = v.T

    pieces = [(half, low, wide) for half in range(HALVES) for low, wide in chunks(OUTER_WIDTHS)]

    def product(half, low, wide):
        own = slice(half * HALF_COLS, (half + 1) * HALF_COLS)
        span = slice(low, low + wide)
        scores = dot(k_ref[:, own], q_block[half, :, span]) * (SCALE * LOG2E)
        scores = scores + bias[half, :, span]
        return scores, jnp.max(scores, axis=0, keepdims=True)

    ones = jnp.ones((RANK, TOK), bf16)
    ahead = product(*pieces[0])
    for at, (half, low, wide) in enumerate(pieces):
        span = slice(low, low + wide)
        scores, top = ahead
        power = jnp.exp2(scores - top)
        probs = power.astype(bf16)
        p_out[0, half, :, span] = probs
        if at + 1 < len(pieces):
            ahead = product(*pieces[at + 1])
        first, last = heads_of(low, wide)
        rows = slice(
            half * HALF_COLS + first * HEAD_DIM, half * HALF_COLS + (last + 1) * HEAD_DIM
        )
        mixed = dot(jnp.concatenate([vt_ref[rows, :], ones], axis=0), probs)
        shrink = 1.0 / mixed[-RANK : 1 - RANK]
        i_flat[half : half + 1, span] = shrink
        o_flat[half, :, span] = pick_heads(mixed, low, wide, first, last) * shrink
    for half in range(HALVES):
        for j in range(HALF_HEADS):
            piece = o_flat[half, :, SLOT * j : SLOT * j + SLOT_W]
            if j:
                piece = pltpu.roll(piece, SLOT_W - 8 * j, 1)
            at = half * HALF_COLS + j * HEAD_DIM
            o_t[at : at + HEAD_DIM, :] = piece
            piece = i_flat[half : half + 1, SLOT * j : SLOT * j + SLOT_W]
            if j:
                piece = pltpu.roll(piece, SLOT_W - 8 * j, 1)
            i_t[half * HALF_HEADS + j : half * HALF_HEADS + j + 1, :] = piece
    o_tb = o_t[...].astype(bf16)
    o = o_tb.T[0:TOK]

    u2 = dot(t_out[mine, :], o_tb[:, 0:TOK]).astype(bf16)
    x1 = x + dot(o, m_out[0:D, :]) + b_out[...]
    normed2, inverse2 = norm_parts(x1)
    h2 = (normed2 * gain2[...] + shift2[...]).astype(bf16)
    u3 = dot_t(t_exp[mine, :], h2).astype(bf16)
    dz = g_ref[0]
    g = dz.astype(f32)
    du4 = dot_t(u_red[mine, :], dz).astype(bf16)
    z = x1 + b_red[...]
    dh2 = jnp.zeros((TOK, D), f32)
    u4 = jnp.zeros((RANK, TOK), f32)
    du3 = jnp.zeros((RANK, TOK), f32)
    for low in range(0, FF, 512):
        span = slice(low, low + 512)
        f = dot(h2, m_exp[:, span]) + b_exp[:, span]
        phi = 0.5 + 0.5 * lax.erf(f * (2.0**-0.5))
        act = (f * phi).astype(bf16)
        slope = phi + f * (jnp.exp2(f * f * (-0.5 * LOG2E)) * 0.3989422804014327)
        da = dot_t(dz, m_red[span, :])
        df = (da * slope).astype(bf16)
        z = z + dot(act, m_red[span, :])
        dh2 = dh2 + dot_t(df, m_exp[:, span])
        u4 = u4 + dot_t(t_red[mine, span], act)
        du3 = du3 + dot_t(u_exp[mine, span], df)
        acc_dr[mine, span] += dot(du4, act)
        acc_ue[mine, span] += dot(u3, df)
    block_out[0] = z.astype(bf16)
    acc_ur[mine, :] += dot(u4.astype(bf16), dz)
    acc_de[mine, :] += dot(du3.astype(bf16), h2)
    dx1 = g + norm_back(dh2, gain2[...], normed2, inverse2)
    dx1_out[0] = dx1
    dy = dx1.astype(bf16)
    acc_uo[mine, :] += dot(u2, dy)
    packed = dot_t(m_out[...], dy)
    du2 = packed[D : D + RANK].astype(bf16)
    acc_do[mine, :] += dot(du2, o)
    d_ot = widen(packed[0:D]).reshape(HEADS, HEAD_DIM, SLOT_W) * i_t[...][:, None, :]
    sums = jnp.sum(d_ot * o_t[...].reshape(HEADS, HEAD_DIM, SLOT_W), axis=1)
    dot_out[0] = d_ot.reshape(D, SLOT_W).astype(bf16)
    row_out[0] = sums

    @pl.when(step == pl.num_programs(0) - 1)
    def _():
        pack_sums(
            sums_out, members, (acc_do, acc_uo, acc_de, acc_ue, acc_dr, acc_ur)
        )


def inner_kernel(
    wins,
    members,
    ids,
    x_ref,
    vectors,
    w_qkv,
    d_qkv,
    u_qkv,
    p_ref,
    qt_ref,
    kt_ref,
    v_ref,
    dot_ref,
    row_ref,
    dx1_ref,
    h1_ref,
    u1_ref,
    grad_out,
    sums_out,
    acc_dq,
    acc_uq,
    m_qkv,
    q_block,
    o_block,
    ds_ref,
    dq_flat,
    dq_t,
    row_flat,
    dqkv,
):
    step = pl.program_id(0)
    adapter = ids[step // wins]
    mine = pl.ds(pl.multiple_of(adapter * RANK, RANK), RANK)

    @pl.when(step == 0)
    def _():
        q_block[...] = jnp.zeros_like(q_block)
        o_block[...] = jnp.zeros_like(o_block)
        acc_dq[...] = jnp.zeros_like(acc_dq)
        acc_uq[...] = jnp.zeros_like(acc_uq)

    @pl.when(lax.rem(step, wins) == 0)
    def _():
        merge(w_qkv, d_qkv, u_qkv, m_qkv, adapter)

    row_flat[...] = jnp.zeros_like(row_flat)
    for half in range(HALVES):
        own = slice(half * HALF_COLS, (half + 1) * HALF_COLS)
        spread_heads(qt_ref[0, own, :], q_block, half)
        spread_heads(dot_ref[0, own, :], o_block, half)
        for j in range(HALF_HEADS):
            at = half * HALF_HEADS + j
            piece = row_ref[0, at : at + 1, :]
            if j:
                piece = pltpu.roll(piece, 8 * j, 1)
            row_flat[half : half + 1, SLOT * j : SLOT * j + SLOT_W] += piece

    pieces = [(half, low, wide) for half in range(HALVES) for low, wide in chunks(INNER_WIDTHS)]
    per_half = len(pieces) // HALVES

    def product(half, low, wide):
        own = slice(half * HALF_COLS, (half + 1) * HALF_COLS)
        return dot(v_ref[0, :, own], o_block[half, :, low : low + wide])

    def queries(half, low, wide, d_scores):
        span = slice(low, low + wide)
        first, last = heads_of(low, wide)
        rows = slice(
            half * HALF_COLS + first * HEAD_DIM, half * HALF_COLS + (last + 1) * HEAD_DIM
        )
        dq_flat[half, :, span] = pick_heads(
            dot(kt_ref[0, rows, :], d_scores), low, wide, first, last
        )

    def values(half):
        at = slice(2 * D + half * HALF_COLS, 2 * D + (half + 1) * HALF_COLS)
        dqkv[:, at] = dot_t(p_ref[0, half], o_block[half]).astype(bf16)

    def keys(half):
        at = slice(D + half * HALF_COLS, D + (half + 1) * HALF_COLS)
        dqkv[:, at] = (dot_t(ds_ref[half], q_block[half]) * SCALE).astype(bf16)

    ahead = product(*pieces[0])
    for at, (half, low, wide) in enumerate(pieces):
        span = slice(low, low + wide)
        d_probs = ahead
        if at + 1 < len(pieces):
            ahead = product(*pieces[at + 1])
        probs = p_ref[0, half, :, span].astype(f32)
        d_scores = (probs * (d_probs - row_flat[half : half + 1, span])).astype(bf16)
        ds_ref[half, :, span] = d_scores
        queries(half, low, wide, d_scores)
        if (at + 1) % per_half == 0:
            values(half)
            keys(half)
    for half in range(HALVES):
        for j in range(HALF_HEADS):
            piece = dq_flat[half, :, SLOT * j : SLOT * j + SLOT_W] * SCALE
            if j:
                piece = pltpu.roll(piece, SLOT_W - 8 * j, 1)
            at = half * HALF_COLS + j * HEAD_DIM
            dq_t[at : at + HEAD_DIM, :] = piece.astype(bf16)
    dqkv[:, 0:D] = dq_t[...].T[0:TOK]

    whole = dqkv[...]
    acc_uq[mine, :] += dot(u1_ref[0], whole)
    du1 = dot_t(u_qkv[mine, :], whole).astype(bf16)
    acc_dq[mine, :] += dot(du1, h1_ref[0])
    dh1 = dot_t(whole, m_qkv[...])
    normed, inverse = norm_parts(x_ref[0].astype(f32))
    gain1 = unpack_vectors(vectors)[0]
    grad_out[0] = dx1_ref[0] + norm_back(dh1, gain1[...], normed, inverse)

    @pl.when(step == pl.num_programs(0) - 1)
    def _():
        pack_sums(sums_out, members, (acc_dq, acc_uq))


def pack_vectors(vectors):
    total = sum(VECTORS)
    low = 0
    packed = jnp.zeros((total,), f32)
    for item, wide in zip(vectors, VECTORS):
        packed = packed + jnp.pad(item.astype(f32), (low, total - low - wide))
        low += wide
    return packed.reshape(1, total)


def whole_spec(shape):
    return pl.BlockSpec(shape, lambda i, ids: (0,) * len(shape), pipeline_mode=pl.Buffered(1))


def step_spec(shape):
    return pl.BlockSpec((1,) + shape, lambda i, ids: (i,) + (0,) * len(shape))


PER_STEP = (
    ((TOK, D), bf16),
    ((HALVES, TOK, LANES), bf16),
    ((D, SLOT_W), bf16),
    ((D, TOK), bf16),
    ((TOK, D), bf16),
    ((D, SLOT_W), bf16),
    ((HEADS, SLOT_W), f32),
    ((TOK, D), f32),
    ((TOK, D), bf16),
    ((RANK, TOK), bf16),
)


def outer_pass(wins, members, tokens, grads, ids, vectors, weights, adapters, bias):
    groups = tokens.shape[0]
    fixed = (vectors, *weights, *adapters, bias)
    rows = sum(down + up for down, up in OUTER)
    return pl.pallas_call(
        functools.partial(outer_kernel, wins, members),
        grid_spec=pltpu.PrefetchScalarGridSpec(
            num_scalar_prefetch=1,
            grid=(groups,),
            in_specs=[step_spec((TOK, D))] * 2 + [whole_spec(item.shape) for item in fixed],
            out_specs=[step_spec(shape) for shape, _ in PER_STEP] + [whole_spec((rows, 128))],
            scratch_shapes=[pltpu.VMEM((COLS, wide), f32) for pair in OUTER for wide in pair]
            + [
                pltpu.VMEM((D, 3 * D), bf16),
                pltpu.VMEM((D + RANK, D), bf16),
                pltpu.VMEM((D, FF), bf16),
                pltpu.VMEM((FF, D), bf16),
                pltpu.VMEM((COLS, D), bf16),
                pltpu.VMEM((COLS, D), bf16),
                pltpu.VMEM((COLS, D), bf16),
                pltpu.VMEM((COLS, FF), bf16),
                pltpu.VMEM((HALVES, HALF_COLS, LANES), bf16),
                pltpu.VMEM((D, SLOT_W), f32),
                pltpu.VMEM((HALVES, HEAD_DIM, LANES), f32),
                pltpu.VMEM((HALVES, LANES), f32),
                pltpu.VMEM((HEADS, SLOT_W), f32),
                pltpu.VMEM((TOK, D), bf16),
                pltpu.VMEM((D, TOK), bf16),
            ],
        ),
        out_shape=[jax.ShapeDtypeStruct((groups,) + shape, kind) for shape, kind in PER_STEP]
        + [jax.ShapeDtypeStruct((rows, 128), f32)],
        compiler_params=pltpu.CompilerParams(vmem_limit_bytes=63 << 20),
        name="outer_pass",
    )(ids, tokens, grads, *fixed)


def inner_pass(wins, members, tokens, ids, vectors, weight, down, up, kept):
    groups = tokens.shape[0]
    fixed = (vectors, weight, down, up)
    rows = sum(first + second for first, second in INNER)
    return pl.pallas_call(
        functools.partial(inner_kernel, wins, members),
        grid_spec=pltpu.PrefetchScalarGridSpec(
            num_scalar_prefetch=1,
            grid=(groups,),
            in_specs=[step_spec((TOK, D))]
            + [whole_spec(item.shape) for item in fixed]
            + [step_spec(shape) for shape, _ in PER_STEP[1:]],
            out_specs=[step_spec((TOK, D)), whole_spec((rows, 128))],
            scratch_shapes=[
                pltpu.VMEM((COLS, D), f32),
                pltpu.VMEM((COLS, 3 * D), f32),
                pltpu.VMEM((D, 3 * D), bf16),
                pltpu.VMEM((HALVES, HALF_COLS, LANES), bf16),
                pltpu.VMEM((HALVES, HALF_COLS, LANES), bf16),
                pltpu.VMEM((HALVES, TOK, LANES), bf16),
                pltpu.VMEM((HALVES, HEAD_DIM, LANES), f32),
                pltpu.VMEM((D, SLOT_W), bf16),
                pltpu.VMEM((HALVES, LANES), f32),
                pltpu.VMEM((TOK, 3 * D), bf16),
            ],
        ),
        out_shape=[
            jax.ShapeDtypeStruct((groups, TOK, D), f32),
            jax.ShapeDtypeStruct((rows, 128), f32),
        ],
        compiler_params=pltpu.CompilerParams(vmem_limit_bytes=63 << 20),
        cost_estimate=pl.CostEstimate(
            flops=groups * 4_000_000_000, bytes_accessed=groups * 12_000_000, transcendentals=0
        ),
        name="inner_pass",
    )(ids, tokens, *fixed, *kept)


def greet(axis, me, size):
    barrier = pltpu.get_barrier_semaphore()
    for hop in range(1, size):
        peer = lax.rem(me + hop, size)
        pl.semaphore_signal(
            barrier, inc=1, device_id={axis: peer}, device_id_type=pl.DeviceIdType.MESH
        )
    return size - 1


def share_kernel(members, count, *refs):
    shards, refs = refs[:count], refs[count:]
    table_ref, select_ref, refs = refs[0], refs[1], refs[2:]
    full, refs = refs[:count], refs[count:]
    bias_out, refs = refs[0], refs[1:]
    held, refs = refs[:count], refs[count:]
    bias, rows_ref, send_sem, recv_sem, out_sem, bias_sem = refs
    me = lax.axis_index("fsdp")
    waits = greet("fsdp", me, members)
    for shard, whole in zip(shards, held):
        rows = shard.shape[0]
        whole[pl.ds(pl.multiple_of(me * rows, rows), rows), :] = shard[...]
    pl.semaphore_wait(pltpu.get_barrier_semaphore(), waits)
    copies = []
    for at, (shard, whole) in enumerate(zip(shards, held)):
        rows = shard.shape[0]
        for hop in range(1, members):
            copy = pltpu.make_async_remote_copy(
                src_ref=shard,
                dst_ref=whole.at[pl.ds(pl.multiple_of(me * rows, rows), rows), :],
                send_sem=send_sem.at[at, hop],
                recv_sem=recv_sem.at[at, hop],
                device_id={"fsdp": lax.rem(me + hop, members)},
                device_id_type=pl.DeviceIdType.MESH,
            )
            copy.start()
            copies.append(copy)
    bias_rows(table_ref, select_ref, rows_ref)
    outs = []
    for half in range(HALVES):
        bias_half(rows_ref, bias, half)
        out = pltpu.make_async_copy(bias.at[half], bias_out.at[half], bias_sem.at[half])
        out.start()
        outs.append(out)
    for copy in copies:
        copy.wait()
    for at, (whole, target) in enumerate(zip(held, full)):
        out = pltpu.make_async_copy(whole, target, out_sem.at[at])
        out.start()
        outs.append(out)
    for out in outs:
        out.wait()


def share_weights(shards, rel_table, members):
    count = len(shards)
    wholes = [(item.shape[0] * members, item.shape[1]) for item in shards]
    outs = pl.pallas_call(
        functools.partial(share_kernel, members, count),
        in_specs=[pl.BlockSpec(memory_space=pltpu.VMEM)] * (count + 2),
        out_specs=[pl.BlockSpec(memory_space=pl.ANY)] * (count + 1),
        out_shape=[jax.ShapeDtypeStruct(shape, bf16) for shape in wholes]
        + [jax.ShapeDtypeStruct((HALVES, TOK, LANES), f32)],
        scratch_shapes=[pltpu.VMEM(shape, bf16) for shape in wholes]
        + [
            pltpu.VMEM((HALVES, TOK, LANES), f32),
            pltpu.VMEM((6, SPATIAL * HEADS, 128), f32),
            pltpu.SemaphoreType.DMA((count, members)),
            pltpu.SemaphoreType.DMA((count, members)),
            pltpu.SemaphoreType.DMA((count,)),
            pltpu.SemaphoreType.DMA((HALVES,)),
        ],
        compiler_params=pltpu.CompilerParams(
            collective_id=0, has_side_effects=True, vmem_limit_bytes=62 << 20
        ),
        name="share_weights",
    )(*shards, rel_table, select_rows())
    return outs[:count], outs[count]


def total_kernel(
    members, copies, sums, out, own, low, first, second, third, piece, sems, s2, r2, s3, r3
):
    mine = lax.axis_index("fsdp")
    place = lax.axis_index("rep")
    waits = greet("fsdp", mine, members)
    waits += greet("rep", place, copies)
    low[...] = sums[...].astype(bf16)
    pl.semaphore_wait(pltpu.get_barrier_semaphore(), waits)
    moves = []
    for hop in range(1, members):
        peer = lax.rem(mine + hop, members)
        move = pltpu.make_async_remote_copy(
            src_ref=low.at[peer],
            dst_ref=first.at[hop - 1],
            send_sem=sems.at[0, hop],
            recv_sem=sems.at[1, hop],
            device_id={"fsdp": peer},
            device_id_type=pl.DeviceIdType.MESH,
        )
        move.start()
        moves.append(move)
    for move in moves:
        move.wait()
    total = sums[mine]
    for hop in range(1, members):
        total = total + first[hop - 1].astype(f32)
    own[...] = total.astype(bf16)
    moves = []
    for hop in range(1, copies):
        peer = lax.rem(place + hop, copies)
        move = pltpu.make_async_remote_copy(
            src_ref=own.at[peer],
            dst_ref=second.at[hop],
            send_sem=s2.at[hop],
            recv_sem=r2.at[hop],
            device_id={"rep": peer},
            device_id_type=pl.DeviceIdType.MESH,
        )
        move.start()
        moves.append(move)
    for move in moves:
        move.wait()
    total = own[place].astype(f32)
    for hop in range(1, copies):
        total = total + second[hop].astype(f32)
    piece[...] = total.astype(bf16)
    moves = []
    for hop in range(1, copies):
        peer = lax.rem(place + hop, copies)
        move = pltpu.make_async_remote_copy(
            src_ref=piece,
            dst_ref=third.at[hop],
            send_sem=s3.at[hop],
            recv_sem=r3.at[hop],
            device_id={"rep": peer},
            device_id_type=pl.DeviceIdType.MESH,
        )
        move.start()
        moves.append(move)
    out[place] = piece[...].astype(f32)
    for hop, move in enumerate(moves):
        move.wait()
        out[lax.rem(place + copies - hop - 1, copies)] = third[hop + 1].astype(f32)


def total_sums(sums, members, copies):
    rows = sums.shape[0] // (members * copies)
    piece = (rows, 128)
    whole = (copies,) + piece
    out = pl.pallas_call(
        functools.partial(total_kernel, members, copies),
        in_specs=[pl.BlockSpec(memory_space=pltpu.VMEM)],
        out_specs=pl.BlockSpec(memory_space=pltpu.VMEM),
        out_shape=jax.ShapeDtypeStruct(whole, f32),
        scratch_shapes=[
            pltpu.VMEM(whole, bf16),
            pltpu.VMEM((members,) + whole, bf16),
            pltpu.VMEM((members - 1,) + whole, bf16),
            pltpu.VMEM(whole, bf16),
            pltpu.VMEM(whole, bf16),
            pltpu.VMEM(piece, bf16),
            pltpu.SemaphoreType.DMA((2, members)),
            pltpu.SemaphoreType.DMA((copies,)),
            pltpu.SemaphoreType.DMA((copies,)),
            pltpu.SemaphoreType.DMA((copies,)),
            pltpu.SemaphoreType.DMA((copies,)),
        ],
        compiler_params=pltpu.CompilerParams(collective_id=1, has_side_effects=True),
        name="total_sums",
    )(sums.reshape((members,) + whole))
    return out.reshape(copies * rows, 128)


def unpack_kernel(members, member, *refs):
    at = 0
    packed = refs[:2]
    outs = refs[2:]
    for source, pairs in zip(packed, (INNER, OUTER)):
        low = 0
        for down, up in pairs:
            part = down // members
            outs[at][...] = source[low : low + part, :]
            low += part
            part = COLS // members
            for lane in range(0, up, 128):
                outs[at + 1][:, lane : lane + 128] = source[low : low + part, :]
                low += part
            at += 2


def unpack_sums(inner, outer, member, members):
    shapes = []
    for down, up in INNER + OUTER:
        shapes.append((down // members, COLS))
        shapes.append((COLS // members, up))
    return pl.pallas_call(
        functools.partial(unpack_kernel, members),
        grid_spec=pltpu.PrefetchScalarGridSpec(
            num_scalar_prefetch=1,
            grid=(1,),
            in_specs=[
                pl.BlockSpec(inner.shape, lambda i, member: (0, 0)),
                pl.BlockSpec((outer.shape[0] // members, 128), lambda i, member: (member[0], 0)),
            ],
            out_specs=[pl.BlockSpec(shape, lambda i, member: (0, 0)) for shape in shapes],
        ),
        out_shape=[jax.ShapeDtypeStruct(shape, f32) for shape in shapes],
        name="unpack_sums",
    )(member.reshape(1), inner, outer)


def on_device(
    tokens,
    grad_out,
    clip_ids,
    norm1_gain,
    norm1_shift,
    weight_qkv,
    bias_qkv,
    rel_table,
    weight_out,
    bias_out,
    norm2_gain,
    norm2_shift,
    weight_expand,
    bias_expand,
    weight_reduce,
    bias_reduce,
    down_qkv,
    up_qkv,
    down_out,
    up_out,
    down_expand,
    up_expand,
    down_reduce,
    up_reduce,
):
    clips, wins, length, width = tokens.shape
    shape = tokens.shape
    members = lax.axis_size("fsdp")
    copies = lax.axis_size("rep")
    tokens = tokens.reshape(clips * wins, length, width)
    grads = grad_out.reshape(clips * wins, length, width)
    vectors = pack_vectors(
        (
            norm1_gain,
            norm1_shift,
            norm2_gain,
            norm2_shift,
            bias_qkv,
            bias_out,
            bias_expand,
            bias_reduce,
        )
    )
    shards = (
        weight_qkv,
        weight_out,
        weight_expand,
        weight_reduce,
        down_qkv,
        up_qkv,
        down_out,
        up_out,
        down_expand,
        up_expand,
        down_reduce,
        up_reduce,
    )
    full, bias = share_weights(shards, rel_table, members)
    block_out, *kept, outer = outer_pass(
        wins, members, tokens, grads, clip_ids, vectors, full[:4], full[4:], bias
    )
    outer = lax.psum(outer, ("fsdp", "rep"))
    grad_tokens, inner = inner_pass(
        wins, members, tokens, clip_ids, vectors, full[0], full[4], full[5], kept
    )
    inner = total_sums(inner, members, copies)
    shares = unpack_sums(inner, outer, lax.axis_index("fsdp"), members)
    return (block_out.reshape(shape), grad_tokens.reshape(shape), *shares)


def solution(mesh):
    row = P("fsdp", None)
    tokens = P("rep", "fsdp", None, None)
    in_specs = (
        tokens,
        tokens,
        P("rep"),
        P(),
        P(),
        row,
        P(),
        P(),
        row,
        P(),
        P(),
        P(),
        row,
        P(),
        row,
        P(),
    ) + (row,) * 8
    out_specs = (tokens, tokens) + (row,) * 8
    return jax.shard_map(
        on_device, mesh=mesh, in_specs=in_specs, out_specs=out_specs, check_vma=False
    )
```
